512 devices in a mesh: batch: 8 (over y), grp: 64 (over x, z, core).
Axes of the slice: x: 4, y: 8, z: 8, core: 2. Of those that a mesh axis runs over, the one named last changes fastest.
Arguments:
- amps: bfloat16 [24, 64, 1024, 128], P('batch', None, 'grp'), may hold values from -6 to 6
- cycle_inter: bfloat16 [24, 1024, 8, 128], P('batch', 'grp'), may hold values from -0.109375 to 0.109375
- k_irrep: int32 [24], replicated, may hold values from 0 to 7
- i_irrep: int32 [64], replicated, may hold values from 0 to 7
- j_irrep: int32 [8], replicated, may hold values from 0 to 7
- virt_count: int32 [8], replicated, may hold values from 64 to 128, as said below
Outputs:
- cycle_term: bfloat16 [64, 8, 1024, 128], P(None, 'batch', 'grp')
The draws below stay inside these ranges and needn't reach their ends.
Inputs may be any that keep to these rules, and one draw needn't show every extreme that they name: `virt_count`: together the counts are 800.
All inputs are finite; a program needn't handle non-finite values.
Results may differ from the reference program's by a relative error of at most 0.013.
Values may be sent and summed in bfloat16 or wider, within the bound.
A program may use at most 64 MiB of HBM per device.

```python
import jax
import jax.numpy as jnp
from jax import lax

NIRREP = 8
SLOTS = 128
VS = 1024
OW = 64
J = 8
KB = 3
K = 24
N_BATCH = 8


def draw_virt_count(key, part):
    table = jnp.array([16, 8, 14, 11, 13, 12, 15, 11], jnp.int32) * (SLOTS // 16)
    order = jax.random.permutation(jax.random.fold_in(key, 11), 8)
    values = table[order]
    first = values[0::2]
    second = values[1::2]
    half = SLOTS // 2
    limit = jnp.minimum(jnp.minimum(SLOTS - first, first - half), jnp.minimum(SLOTS - second, second - half))
    shift = jax.random.randint(jax.random.fold_in(key, 23), (4,), -limit, limit + 1)
    paired = jnp.stack([first + shift, second - shift], axis=1)
    return paired.reshape(8).astype(jnp.int32)


def with_ends(values, key, least, top_value):
    extent = values.shape
    index_at = [jax.random.randint(jax.random.fold_in(key, axis), (), 0, extent[axis]) for axis in range(len(extent))]
    values = values.at[tuple(index_at)].set(least)
    longest = extent.index(max(extent))
    index_at[longest] = (index_at[longest] + 1) % extent[longest]
    return values.at[tuple(index_at)].set(top_value)


def shard_levels(rng, dims, split, least, largest):
    def one(dim, shards_of):
        steps = jax.random.uniform(jax.random.fold_in(jax.random.fold_in(rng, 6), dim), (shards_of,), jnp.float32, least / len(split), largest / len(split))
        return jnp.repeat(jnp.exp(steps), dims[dim] // shards_of).reshape((-1,) + (1,) * (len(dims) - dim - 1))

    gain = one(*split[0])
    for cut in split[1:]:
        gain = gain * one(*cut)
    return gain


def centred(rng, dims, deviation, reach, shards=(), held_as=jnp.bfloat16):
    values = jax.random.normal(rng, dims, jnp.float32) * deviation
    if len(shards) > 0:
        values = shard_levels(rng, dims, shards, -0.22, 0.18) * values
    return jnp.clip(values, min=-reach, max=reach).astype(held_as)


def setup_inputs(seed: int = 0) -> dict:
    splits = jax.random.split(jax.random.key(seed), 7)
    amps = centred(splits[0], (K, OW, VS, SLOTS), 1.0, 6.0, ((0, 8), (2, 64)))
    cycle_inter = centred(splits[1], (K, VS, J, SLOTS), (K * SLOTS) ** -0.5, 0.109375, ((0, 8), (1, 64)))
    k_irrep = with_ends(jax.random.randint(splits[2], (K,), 0, 8), jax.random.fold_in(splits[2], 1), 0, 7).astype(jnp.int32)
    i_irrep = with_ends(jax.random.randint(splits[3], (OW,), 0, 8), jax.random.fold_in(splits[3], 1), 0, 7).astype(jnp.int32)
    j_irrep = with_ends(jax.random.randint(splits[4], (J,), 0, 8), jax.random.fold_in(splits[4], 1), 0, 7).astype(jnp.int32)
    virt_count = draw_virt_count(jax.random.fold_in(splits[6], 71), 0)
    return dict(amps=amps, cycle_inter=cycle_inter, k_irrep=k_irrep, i_irrep=i_irrep, j_irrep=j_irrep, virt_count=virt_count)


def reference(amps, cycle_inter, k_irrep, i_irrep, j_irrep, virt_count):
    irreps = jnp.arange(NIRREP, dtype=jnp.int32)
    slot_pos = jnp.arange(SLOTS, dtype=jnp.int32)
    slot_index = jnp.arange(VS, dtype=jnp.int32)
    c_labels = slot_index // SLOTS
    c_live = (slot_index % SLOTS) < virt_count[c_labels]
    total = jnp.zeros((OW, J, VS, SLOTS), jnp.float32)
    for group in range(N_BATCH):
        partial_value = jnp.zeros((OW, J, NIRREP, SLOTS, SLOTS), jnp.float32)
        for local in range(KB):
            index = group * KB + local
            label = k_irrep[index]
            flip = jnp.bitwise_xor(label, i_irrep)
            a_labels = jnp.bitwise_xor(flip[:, None], c_labels[None, :])
            amp_mask = c_live[None, :, None] & (slot_pos[None, None, :] < virt_count[a_labels][:, :, None])
            amp_k = jnp.where(amp_mask, amps[index], jnp.zeros((), amps.dtype)).astype(jnp.float32)
            b_labels = jnp.bitwise_xor(jnp.bitwise_xor(label, c_labels)[:, None], j_irrep[None, :])
            inter_mask = c_live[:, None, None] & (slot_pos[None, None, :] < virt_count[b_labels][:, :, None])
            inter_k = jnp.where(inter_mask, cycle_inter[index], jnp.zeros((), cycle_inter.dtype)).astype(jnp.float32)
            products = jnp.einsum("inca,ncjb->ijnab", amp_k.reshape(OW, NIRREP, SLOTS, SLOTS), inter_k.reshape(NIRREP, SLOTS, J, SLOTS))
            source = jnp.bitwise_xor(irreps[None, :], flip[:, None]).astype(jnp.int32)
            partial_value = partial_value + jnp.take_along_axis(products, source[:, None, :, None, None], axis=2)
        rounded = lax.optimization_barrier(partial_value.reshape(OW, J, VS, SLOTS).astype(jnp.bfloat16))
        total = total + rounded.astype(jnp.float32)
    return total.astype(jnp.bfloat16)
```

```python
import jax
import jax.numpy as jnp
from jax import lax
from jax.sharding import PartitionSpec as P


def shards(amps, cycle_inter, k_irrep, i_irrep, j_irrep, virt_count):
    k_local = amps.shape[0]
    slab_size = amps.shape[2]
    width = amps.shape[3]
    n_irrep = virt_count.shape[0]
    j_total = cycle_inter.shape[2]
    irreps = jnp.arange(n_irrep, dtype=jnp.int32)
    slot_pos = jnp.arange(width, dtype=jnp.int32)

    def count_of(labels):
        return jnp.sum(jnp.where(labels[..., None] == irreps, virt_count, 0), axis=-1)

    k_first = lax.axis_index("batch") * k_local
    k_labels = lax.dynamic_slice_in_dim(k_irrep, k_first, k_local)
    c_index = lax.axis_index("grp") * slab_size + jnp.arange(slab_size, dtype=jnp.int32)
    c_labels = c_index // width
    c_live = c_index % width < count_of(c_labels)
    a_labels = jnp.bitwise_xor(
        jnp.bitwise_xor(k_labels[:, None, None], i_irrep[None, :, None]), c_labels[None, None, :]
    )
    amp_mask = c_live[None, None, :, None] & (slot_pos < count_of(a_labels)[..., None])
    masked_amps = jnp.where(amp_mask, amps, jnp.zeros((), amps.dtype))
    b_labels = jnp.bitwise_xor(
        jnp.bitwise_xor(k_labels[:, None, None], c_labels[None, :, None]), j_irrep[None, None, :]
    )
    inter_mask = c_live[None, :, None, None] & (slot_pos < count_of(b_labels)[..., None])
    masked_inter = jnp.where(inter_mask, cycle_inter, jnp.zeros((), cycle_inter.dtype))
    sorted_amps = lax.all_to_all(masked_amps, "grp", split_axis=1, concat_axis=2, tiled=True)
    whole_inter = lax.all_gather(masked_inter, "grp", axis=1, tiled=True)
    i_count = sorted_amps.shape[1]
    i_labels = lax.dynamic_slice_in_dim(i_irrep, lax.axis_index("grp") * i_count, i_count)
    k_source = jnp.bitwise_xor(irreps[None, :], k_labels[:, None])
    amp_blocks = sorted_amps.reshape(k_local, i_count, n_irrep, width, width)
    amp_perm = jnp.take_along_axis(amp_blocks, k_source[:, None, :, None, None], axis=2)
    inter_blocks = whole_inter.reshape(k_local, n_irrep, width, j_total, width)
    inter_perm = jnp.take_along_axis(inter_blocks, k_source[:, :, None, None, None], axis=1)
    products = jnp.einsum(
        "kiqca,kqcjb->iqajb", amp_perm, inter_perm, preferred_element_type=jnp.float32
    )
    i_source = jnp.bitwise_xor(irreps[None, :], i_labels[:, None])
    partial_value = jnp.take_along_axis(products, i_source[:, :, None, None, None], axis=1)
    partial_value = jnp.transpose(partial_value, (0, 3, 1, 2, 4)).reshape(
        i_count, j_total, n_irrep * width, width
    )
    rounded = partial_value.astype(jnp.bfloat16)
    summed = lax.psum_scatter(rounded, "batch", scatter_dimension=1, tiled=True)
    outgoing = summed.reshape(-1, slab_size, width)
    arrived = lax.all_to_all(outgoing, "grp", split_axis=0, concat_axis=0, tiled=True)
    return arrived.reshape(-1, 1, slab_size, width)


def solution(mesh):
    return jax.shard_map(
        shards,
        mesh=mesh,
        in_specs=(P("batch", None, "grp", None), P("batch", "grp", None, None), P(), P(), P(), P()),
        out_specs=P(None, "batch", "grp", None),
        check_vma=False,
    )
```

```python
import jax
import jax.numpy as jnp
from jax import lax
from jax.experimental import pallas as pl
from jax.experimental.pallas import tpu as pltpu
from jax.sharding import PartitionSpec as P

MESH = pl.DeviceIdType.MESH
NX, NZ, NC = 4, 8, 2


def gather_kernel(src, out, local_sem, send, recv):
    y, g = lax.axis_index("batch"), lax.axis_index("grp")
    core = lax.rem(g, NC)
    z = lax.rem(lax.div(g, NC), NZ)
    x = lax.div(g, NC * NZ)
    other = 1 - core

    def dev(xx, zz, cc):
        return (y, (xx * NZ + zz) * NC + cc)

    def xo(d):
        return lax.rem(x + d + NX, NX)

    def zo(d):
        return lax.rem(z + d + NZ, NZ)

    half = src.shape[1] // 2
    low, high = pl.ds(0, half), pl.ds(half, half)
    used = [0]

    def copy(view, at, target):
        n = used[0]
        used[0] += 1
        c = pltpu.make_async_remote_copy(
            src_ref=view, dst_ref=at, send_sem=send.at[n], recv_sem=recv.at[n], device_id=target, device_id_type=MESH
        )
        c.start()
        return c

    partners = [dev(xo(d), z, core) for d in range(1, NX)]
    partners += [dev(x, zo(d), core) for d in range(1, NZ)]
    partners += [dev(x, z, other)]
    own = pltpu.make_async_copy(src, out.at[:, x, z, core], local_sem)
    own.start()
    barrier = pltpu.get_barrier_semaphore()
    for p in partners:
        pl.semaphore_signal(barrier, inc=1, device_id=p, device_id_type=MESH)
    pl.semaphore_wait(barrier, len(partners))

    started = []

    def go(view, at, target):
        c = copy(view, at, target)
        started.append(c)
        return c

    def same(ref, target):
        return go(ref, ref, target)

    mate = dev(x, z, other)
    along_x = [go(src.at[:, low], out.at[:, x, z, core, low], dev(xo(d), z, core)) for d in range(1, NX)]
    along_z = [go(src.at[:, high], out.at[:, x, z, core, high], dev(x, zo(d), core)) for d in range(1, NZ)]
    own.wait()

    def row(zz):
        return out.at[:, :, zz, core, low]

    def row_part(zz, part):
        return out.at[:, pl.ds(part * (NX // 2), NX // 2), zz, core, low]

    def col(xx):
        return out.at[:, xx, :, core, high]

    def col_part(xx, part):
        return out.at[:, xx, pl.ds(part * (NZ // 2), NZ // 2), core, high]

    mates = []
    zp, zm = dev(x, zo(1), core), dev(x, zo(-1), core)
    xp, xm = dev(xo(1), z, core), dev(xo(-1), z, core)
    for c in along_x:
        c.wait_recv()
    up = same(row(z), zp)
    down = same(row(z), zm)
    mates.append(same(row(z), mate))
    for c in along_z:
        c.wait_recv()
    right = same(col(x), xp)
    left = same(col(x), xm)
    mates.append(same(col(x), mate))
    for s in range(1, NZ // 2):
        last = s == NZ // 2 - 1
        up.wait_recv()
        up_next = same(row_part(zo(-s), 0) if last else row(zo(-s)), zp)
        down.wait_recv()
        down_next = same(row_part(zo(s), 1) if last else row(zo(s)), zm)
        mates.append(same(row(zo(-s)), mate))
        mates.append(same(row(zo(s)), mate))
        up, down = up_next, down_next
        if s == 2:
            right.wait_recv()
            right2 = same(col_part(xo(-1), 0), xp)
            left.wait_recv()
            left2 = same(col_part(xo(1), 1), xm)
            mates.append(same(col(xo(-1)), mate))
            mates.append(same(col(xo(1)), mate))
    right2.wait_recv()
    left2.wait_recv()
    mates.append(same(col(xo(2)), mate))
    up.wait_recv()
    down.wait_recv()
    mates.append(same(row(zo(NZ // 2)), mate))
    for c in mates:
        c.wait_recv()
    for c in started:
        c.wait_send()


COPIES = 34


def gather(block):
    k, j, c, b = block.shape
    return pl.pallas_call(
        gather_kernel,
        out_shape=jax.ShapeDtypeStruct((k, NX, NZ, NC, j, c, b), block.dtype),
        in_specs=[pl.BlockSpec(memory_space=pltpu.VMEM)],
        out_specs=pl.BlockSpec(memory_space=pl.ANY),
        scratch_shapes=[
            pltpu.SemaphoreType.DMA,
            pltpu.SemaphoreType.DMA((COPIES,)),
            pltpu.SemaphoreType.DMA((COPIES,)),
        ],
        compiler_params=pltpu.CompilerParams(collective_id=0, has_side_effects=True),
        cost_estimate=pl.CostEstimate(flops=0, bytes_accessed=12 << 20, transcendentals=0),
    )(block)


def product_kernel(flips, *refs):
    n = (len(refs) - 1) // 2
    out = refs[-1]
    lhs = jnp.concatenate([r[0, 0].reshape(-1, r.shape[-1]) for r in refs[:n]], axis=0)
    rhs = refs[n:-1]
    js = out.shape[0]
    for j in range(0, js, 2):
        cols = [
            jnp.concatenate([r[0, 0, :, jj].reshape(-1, r.shape[-1]) for r in rhs], axis=0) for jj in (j, j + 1)
        ]
        both = lax.dot_general(
            lhs, jnp.concatenate(cols, axis=1), (((0,), (0,)), ((), ())), preferred_element_type=jnp.float32
        )
        w = both.shape[1] // 2
        out[j] = both[:, :w].astype(out.dtype)
        out[j + 1] = both[:, w:].astype(out.dtype)


def product(flips, amps, inter):
    k, n, sub, c, a = amps.shape
    j, b = inter.shape[3], inter.shape[5]

    def amp_spec(kk):
        return pl.BlockSpec((1, 1, sub, c, a), lambda r, f: (kk, r ^ f[kk], 0, 0, 0))

    def inter_spec(kk):
        return pl.BlockSpec((1, 1, sub, j, c, b), lambda r, f: (kk, r ^ f[kk], 0, 0, 0, 0))

    return pl.pallas_call(
        product_kernel,
        out_shape=jax.ShapeDtypeStruct((j, n * a, b), jnp.bfloat16),
        grid_spec=pltpu.PrefetchScalarGridSpec(
            num_scalar_prefetch=1,
            grid=(n,),
            in_specs=[amp_spec(kk) for kk in range(k)] + [inter_spec(kk) for kk in range(k)],
            out_specs=pl.BlockSpec((j, a, b), lambda r, f: (0, r, 0)),
        ),
        cost_estimate=pl.CostEstimate(flops=2 * k * n * sub * c * a * j * b, bytes_accessed=9 << 20, transcendentals=0),
    )(flips, *([amps] * k), *([inter] * k))


def shards(amps, cycle_inter, k_irrep, i_irrep, j_irrep, virt_count):
    k_local = amps.shape[0]
    slab_size = amps.shape[2]
    width = amps.shape[3]
    n_irrep = virt_count.shape[0]
    j_total = cycle_inter.shape[2]
    irreps = jnp.arange(n_irrep, dtype=jnp.int32)
    slot_pos = jnp.arange(width, dtype=jnp.int32)

    def count_of(labels):
        return jnp.sum(jnp.where(labels[..., None] == irreps, virt_count, 0), axis=-1)

    grp = lax.axis_index("grp")
    k_first = lax.axis_index("batch") * k_local
    k_labels = lax.dynamic_slice_in_dim(k_irrep, k_first, k_local)
    c_label = grp * slab_size // width
    c_pos = grp * slab_size % width + jnp.arange(slab_size, dtype=jnp.int32)
    c_live = c_pos < count_of(c_label)
    a_counts = count_of(k_labels[:, None] ^ i_irrep[None, :] ^ c_label)
    amp_mask = c_live[None, None, :, None] & (slot_pos < a_counts[:, :, None, None])
    masked_amps = jnp.where(amp_mask, amps, jnp.zeros((), amps.dtype))
    b_counts = count_of(k_labels[:, None] ^ j_irrep[None, :] ^ c_label)
    inter_mask = c_live[None, None, :, None] & (slot_pos < b_counts[:, :, None, None])
    turned = jnp.transpose(cycle_inter, (0, 2, 1, 3))
    masked_inter = jnp.where(inter_mask, turned, jnp.zeros((), cycle_inter.dtype))
    sorted_amps = lax.all_to_all(masked_amps, "grp", split_axis=1, concat_axis=1, tiled=True)
    whole_inter = gather(masked_inter)
    i_label = lax.dynamic_index_in_dim(i_irrep, grp, keepdims=False)
    sub = width // slab_size
    partial = product(
        k_labels ^ i_label,
        sorted_amps.reshape(k_local, n_irrep, sub, slab_size, width),
        whole_inter.reshape(k_local, n_irrep, sub, j_total, slab_size, width),
    )
    summed = lax.psum_scatter(partial, "batch", scatter_dimension=0, tiled=True)
    outgoing = summed.reshape(-1, slab_size, width)
    arrived = lax.all_to_all(outgoing, "grp", split_axis=0, concat_axis=0, tiled=True)
    return arrived.reshape(-1, 1, slab_size, width)


def solution(mesh):
    return jax.shard_map(
        shards,
        mesh=mesh,
        in_specs=(P("batch", None, "grp", None), P("batch", "grp", None, None), P(), P(), P(), P()),
        out_specs=P(None, "batch", "grp", None),
        check_vma=False,
    )
```

```python
import jax
import jax.numpy as jnp
from jax import lax
from jax.experimental import pallas as pl
from jax.experimental.pallas import tpu as pltpu
from jax.sharding import PartitionSpec as P

MESH = pl.DeviceIdType.MESH
NX, NZ, NC = 4, 8, 2


def gather_kernel(src, out, local_sem, send, recv):
    y, g = lax.axis_index("batch"), lax.axis_index("grp")
    core = lax.rem(g, NC)
    z = lax.rem(lax.div(g, NC), NZ)
    x = lax.div(g, NC * NZ)
    other = 1 - core

    def dev(xx, zz, cc):
        return (y, (xx * NZ + zz) * NC + cc)

    def xo(d):
        return lax.rem(x + d + NX, NX)

    def zo(d):
        return lax.rem(z + d + NZ, NZ)

    half = src.shape[1] // 2
    low, high = pl.ds(0, half), pl.ds(half, half)
    used = [0]

    def copy(view, at, target):
        n = used[0]
        used[0] += 1
        c = pltpu.make_async_remote_copy(
            src_ref=view, dst_ref=at, send_sem=send.at[n], recv_sem=recv.at[n], device_id=target, device_id_type=MESH
        )
        c.start()
        return c

    partners = [dev(xo(d), z, core) for d in range(1, NX)]
    partners += [dev(x, zo(d), core) for d in range(1, NZ)]
    partners += [dev(x, z, other)]
    own = pltpu.make_async_copy(src, out.at[:, x, z, core], local_sem)
    own.start()
    barrier = pltpu.get_barrier_semaphore()
    for p in partners:
        pl.semaphore_signal(barrier, inc=1, device_id=p, device_id_type=MESH)
    pl.semaphore_wait(barrier, len(partners))

    started = []

    def go(view, at, target):
        c = copy(view, at, target)
        started.append(c)
        return c

    def same(ref, target):
        return go(ref, ref, target)

    mate = dev(x, z, other)
    along_x = [go(src.at[:, low], out.at[:, x, z, core, low], dev(xo(d), z, core)) for d in range(1, NX)]
    along_z = [go(src.at[:, high], out.at[:, x, z, core, high], dev(x, zo(d), core)) for d in range(1, NZ)]
    own.wait()

    def row(zz):
        return out.at[:, :, zz, core, low]

    def row_part(zz, part):
        return out.at[:, pl.ds(part * (NX // 2), NX // 2), zz, core, low]

    def col(xx):
        return out.at[:, xx, :, core, high]

    def col_part(xx, part):
        return out.at[:, xx, pl.ds(part * (NZ // 2), NZ // 2), core, high]

    mates = []
    zp, zm = dev(x, zo(1), core), dev(x, zo(-1), core)
    xp, xm = dev(xo(1), z, core), dev(xo(-1), z, core)
    for c in along_x:
        c.wait_recv()
    up = same(row(z), zp)
    down = same(row(z), zm)
    mates.append(same(row(z), mate))
    for c in along_z:
        c.wait_recv()
    right = same(col(x), xp)
    left = same(col(x), xm)
    mates.append(same(col(x), mate))
    for s in range(1, NZ // 2):
        last = s == NZ // 2 - 1
        up.wait_recv()
        up_next = same(row_part(zo(-s), 0) if last else row(zo(-s)), zp)
        down.wait_recv()
        down_next = same(row_part(zo(s), 1) if last else row(zo(s)), zm)
        mates.append(same(row(zo(-s)), mate))
        mates.append(same(row(zo(s)), mate))
        up, down = up_next, down_next
        if s == 2:
            right.wait_recv()
            right2 = same(col_part(xo(-1), 0), xp)
            left.wait_recv()
            left2 = same(col_part(xo(1), 1), xm)
            mates.append(same(col(xo(-1)), mate))
            mates.append(same(col(xo(1)), mate))
    right2.wait_recv()
    left2.wait_recv()
    mates.append(same(col(xo(2)), mate))
    up.wait_recv()
    down.wait_recv()
    mates.append(same(row(zo(NZ // 2)), mate))
    for c in mates:
        c.wait_recv()
    for c in started:
        c.wait_send()


COPIES = 34


def gather(block):
    k, j, c, b = block.shape
    return pl.pallas_call(
        gather_kernel,
        out_shape=jax.ShapeDtypeStruct((k, NX, NZ, NC, j, c, b), block.dtype),
        in_specs=[pl.BlockSpec(memory_space=pltpu.VMEM)],
        out_specs=pl.BlockSpec(memory_space=pl.ANY),
        scratch_shapes=[
            pltpu.SemaphoreType.DMA,
            pltpu.SemaphoreType.DMA((COPIES,)),
            pltpu.SemaphoreType.DMA((COPIES,)),
        ],
        compiler_params=pltpu.CompilerParams(collective_id=0, has_side_effects=True),
        cost_estimate=pl.CostEstimate(flops=0, bytes_accessed=12 << 20, transcendentals=0),
    )(block)


def reduce_kernel(k_irrep, i_irrep, j_irrep, counts, amps, inter, out, lhs, part, to_up, at_up, to_down, at_down, *sems):
    send_up, recv_up, send_down, recv_down = sems
    y, g = lax.axis_index("batch"), lax.axis_index("grp")
    n, _, ks, c, a = amps.shape
    rows = amps.shape[1] * c
    ring = inter.shape[3]
    far = ring // 2
    b = inter.shape[5]
    per = n // 2

    def yo(d):
        return lax.rem(y + d + ring, ring)

    barrier = pltpu.get_barrier_semaphore()
    for d in (1, -1):
        pl.semaphore_signal(barrier, inc=1, device_id=(yo(d), g), device_id_type=MESH)

    i_label = i_irrep[g]
    flips = [k_irrep[y * ks + kk] ^ i_label for kk in range(ks)]
    c_pos = lax.broadcasted_iota(jnp.int32, (rows, a), 0)

    def prepare(r, carry):
        for kk in range(ks):
            irrep = r ^ flips[kk]
            block = amps[irrep, :, kk].reshape(rows, a).astype(jnp.float32)
            live = jnp.where(c_pos < counts[irrep], block, 0.0)
            lhs[r, :, kk * rows : (kk + 1) * rows] = live.T.astype(lhs.dtype)
        return carry

    lax.fori_loop(0, n, prepare, 0)

    def right(r, j):
        return jnp.concatenate([inter[kk, r ^ flips[kk], :, j].reshape(rows, b) for kk in range(ks)], axis=0)

    def one(r, j):
        return jnp.dot(lhs[r], right(r, j), preferred_element_type=jnp.float32)

    def two(r, j, jj):
        both = jnp.concatenate([right(r, j), right(r, jj)], axis=1)
        return jnp.dot(lhs[r], both, preferred_element_type=jnp.float32)

    ups, downs = {}, {}

    def send(table, src, dst, send_sem, recv_sem, s, h, step):
        copy = pltpu.make_async_remote_copy(
            src_ref=src.at[s, h],
            dst_ref=dst.at[s, h],
            send_sem=send_sem.at[s, h],
            recv_sem=recv_sem.at[s, h],
            device_id=(yo(step), g),
            device_id_type=MESH,
        )
        copy.start()
        table[s, h] = copy

    def send_upward(s, h):
        send(ups, to_up, at_up, send_up, recv_up, s, h, 1)

    def send_downward(s, h):
        send(downs, to_down, at_down, send_down, recv_down, s, h, -1)

    def first(r, carry):
        to_up[0, 0, r] = one(r, yo(far)).astype(to_up.dtype)
        return carry

    def second(r, carry):
        to_down[0, 1, r] = one(r + per, yo(far)).astype(to_down.dtype)
        return carry

    lax.fori_loop(0, per, first, 0)
    pl.semaphore_wait(barrier, 2)
    send_upward(0, 0)
    lax.fori_loop(0, per, second, 0)
    send_downward(0, 1)

    for s in range(1, far):

        def products(r, carry):
            both = two(r, yo(far - s), yo(s - far))
            part[0, r] = both[:, :b]
            part[1, r] = both[:, b:]
            return carry

        lax.fori_loop(0, n, products, 0)

        def upward(h):
            value = part[0, pl.ds(h * per, per)]
            if (s - 1, h) in ups:
                ups[s - 1, h].wait_recv()
                value = value + at_up[s - 1, h].astype(jnp.float32)
            to_up[s, h] = value.astype(to_up.dtype)
            send_upward(s, h)

        def downward(h):
            value = part[1, pl.ds(h * per, per)]
            if (s - 1, h) in downs:
                downs[s - 1, h].wait_recv()
                value = value + at_down[s - 1, h].astype(jnp.float32)
            to_down[s, h] = value.astype(to_down.dtype)
            send_downward(s, h)

        order = (1, 0) if s == 1 else (0, 1)
        for h in order:
            upward(h)
            downward(1 - h if s == 1 else h)

    def own(r, carry):
        part[0, r] = one(r, y)
        return carry

    lax.fori_loop(0, n, own, 0)
    flip = i_label ^ j_irrep[y]
    a_pos = lax.broadcasted_iota(jnp.int32, (a, b), 0)
    b_pos = lax.broadcasted_iota(jnp.int32, (a, b), 1)
    for h in (1, 0):
        ups[far - 1, h].wait_recv()
        downs[far - 1, h].wait_recv()

        def total(r, carry):
            irrep = r + h * per
            value = part[0, irrep] + at_up[far - 1, h, r].astype(jnp.float32) + at_down[far - 1, h, r].astype(jnp.float32)
            live = (a_pos < counts[irrep]) & (b_pos < counts[irrep ^ flip])
            out[irrep] = jnp.where(live, value, 0.0).astype(out.dtype)
            return carry

        lax.fori_loop(0, per, total, 0)
    for copy in list(ups.values()) + list(downs.values()):
        copy.wait_send()


def reduce(amps, inter, k_irrep, i_irrep, j_irrep, counts):
    n, sub, k, c, a = amps.shape
    j, b = inter.shape[3], inter.shape[5]
    half = (j // 2, 2, n // 2, a, b)
    return pl.pallas_call(
        reduce_kernel,
        out_shape=jax.ShapeDtypeStruct((n, a, b), jnp.bfloat16),
        in_specs=[pl.BlockSpec(memory_space=pltpu.SMEM)] * 4 + [pl.BlockSpec(memory_space=pltpu.VMEM)] * 2,
        out_specs=pl.BlockSpec(memory_space=pltpu.VMEM),
        scratch_shapes=[pltpu.VMEM((n, a, k * sub * c), jnp.bfloat16), pltpu.VMEM((2, n, a, b), jnp.float32)]
        + [pltpu.VMEM(half, jnp.bfloat16)] * 4
        + [pltpu.SemaphoreType.DMA(half[:2])] * 4,
        compiler_params=pltpu.CompilerParams(collective_id=1, has_side_effects=True, vmem_limit_bytes=48 << 20),
        cost_estimate=pl.CostEstimate(flops=2 * k * n * sub * c * a * j * b, bytes_accessed=9 << 20, transcendentals=0),
    )(k_irrep, i_irrep, j_irrep, counts, amps, inter)


def shards(amps, cycle_inter, k_irrep, i_irrep, j_irrep, virt_count):
    k_local, i_total, slab_size, width = amps.shape
    n_irrep = virt_count.shape[0]
    j_total = cycle_inter.shape[2]
    sub = width // slab_size
    sorted_amps = lax.all_to_all(jnp.transpose(amps, (1, 0, 2, 3)), "grp", split_axis=0, concat_axis=0, tiled=True)
    whole_inter = gather(jnp.transpose(cycle_inter, (0, 2, 1, 3)))
    summed = reduce(
        sorted_amps.reshape(n_irrep, sub, k_local, slab_size, width),
        whole_inter.reshape(k_local, n_irrep, sub, j_total, slab_size, width),
        k_irrep,
        i_irrep,
        j_irrep,
        virt_count,
    )
    outgoing = summed.reshape(i_total, slab_size, width)
    arrived = lax.all_to_all(outgoing, "grp", split_axis=0, concat_axis=0, tiled=True)
    return arrived.reshape(i_total, 1, slab_size, width)


def solution(mesh):
    return jax.shard_map(
        shards,
        mesh=mesh,
        in_specs=(P("batch", None, "grp", None), P("batch", "grp", None, None), P(), P(), P(), P()),
        out_specs=P(None, "batch", "grp", None),
        check_vma=False,
    )
```

```python
import jax
import jax.numpy as jnp
from jax import lax
from jax.experimental import pallas as pl
from jax.experimental.pallas import tpu as pltpu
from jax.sharding import PartitionSpec as P

MESH = pl.DeviceIdType.MESH
NX, NZ, NC = 4, 8, 2
GRP = NX * NZ * NC
COPIES = 34


def cycle_kernel(
    k_irrep, i_irrep, j_irrep, counts, amps, src, out,
    low0, low1, low2, low3, high0, high1, high2, high3, sorted_amps, lhs, part, summed, to_up, at_up, to_down, at_down,
    local_sem, send, recv, amp_send, amp_recv, out_send, out_recv, send_up, recv_up, send_down, recv_down,
):
    y, g = lax.axis_index("batch"), lax.axis_index("grp")
    core = lax.rem(g, NC)
    z = lax.rem(lax.div(g, NC), NZ)
    x = lax.div(g, NC * NZ)
    lows, highs = (low0, low1, low2, low3), (high0, high1, high2, high3)
    _, _, _, ks, c, b = low0.shape
    ring = src.shape[0]
    far = ring // 2
    n, a = lhs.shape[:2]
    rows = lhs.shape[2] // ks
    subs = rows // c
    per = n // 2

    def yo(d):
        return lax.rem(y + d + ring, ring)

    def xo(d):
        return lax.rem(x + d + NX, NX)

    def zo(d):
        return lax.rem(z + d + NZ, NZ)

    def dev(xx, zz, cc):
        return (y, (xx * NZ + zz) * NC + cc)

    def low(t):
        return yo(far - t)

    def high(t):
        return y if t == 0 else yo(t - far)

    own_blocks = []
    for t in range(far):
        for side, (j, held) in enumerate(((low(t), lows[t]), (high(t), highs[t]))):
            own_blocks.append(pltpu.make_async_copy(src.at[j], held.at[x, z, core], local_sem.at[2 * t + side]))
    own_amps = pltpu.make_async_copy(amps.at[:, g], sorted_amps.at[g], local_sem.at[ring])
    for copy in own_blocks + [own_amps]:
        copy.start()

    barrier = pltpu.get_barrier_semaphore()

    def greet(d, carry):
        pl.semaphore_signal(barrier, inc=1, device_id=(y, lax.rem(g + d, GRP)), device_id_type=MESH)
        return carry

    lax.fori_loop(1, GRP, greet, 0)
    for d in (1, -1):
        pl.semaphore_signal(barrier, inc=1, device_id=(yo(d), g), device_id_type=MESH)
    pl.semaphore_wait(barrier, GRP + 1)

    started = []

    def go(t, view, at, target):
        table = [p for p in started if p[0] == t]
        at_sem = t * COPIES + len(table)
        copy = pltpu.make_async_remote_copy(
            src_ref=view, dst_ref=at, send_sem=send.at[at_sem], recv_sem=recv.at[at_sem], device_id=target, device_id_type=MESH
        )
        copy.start()
        started.append((t, copy))
        return copy

    def same(t, ref, target):
        return go(t, ref, ref, target)

    def row(t, zz):
        return lows[t].at[:, zz, core]

    def row_part(t, zz, p):
        return lows[t].at[pl.ds(p * (NX // 2), NX // 2), zz, core]

    def col(t, xx):
        return highs[t].at[xx, :, core]

    def col_part(t, xx, p):
        return highs[t].at[xx, pl.ds(p * (NZ // 2), NZ // 2), core]

    mate = dev(x, z, 1 - core)
    zp, zm = dev(x, zo(1), core), dev(x, zo(-1), core)
    xp, xm = dev(xo(1), z, core), dev(xo(-1), z, core)
    state = {}

    def open_chunk(t):
        along_x = [go(t, src.at[low(t)], lows[t].at[x, z, core], dev(xo(d), z, core)) for d in range(1, NX)]
        along_z = [go(t, src.at[high(t)], highs[t].at[x, z, core], dev(x, zo(d), core)) for d in range(1, NZ)]
        state[t] = dict(along_x=along_x, along_z=along_z, mates=[])

    def advance(t, step):
        st = state[t]
        mates = st["mates"]
        if step == 1:
            for copy in st["along_x"]:
                copy.wait_recv()
            st["up"] = same(t, row(t, z), zp)
            st["down"] = same(t, row(t, z), zm)
            for copy in st["along_z"]:
                copy.wait_recv()
            st["right"] = same(t, col(t, x), xp)
            st["left"] = same(t, col(t, x), xm)
            mates.append(same(t, row(t, z), mate))
            mates.append(same(t, col(t, x), mate))
        elif step <= NZ // 2:
            s = step - 1
            last = s == NZ // 2 - 1
            st["up"].wait_recv()
            up = same(t, row_part(t, zo(-s), 0) if last else row(t, zo(-s)), zp)
            st["down"].wait_recv()
            down = same(t, row_part(t, zo(s), 1) if last else row(t, zo(s)), zm)
            mates.append(same(t, row(t, zo(-s)), mate))
            mates.append(same(t, row(t, zo(s)), mate))
            st["up"], st["down"] = up, down
            if s == 2:
                st["right"].wait_recv()
                right = same(t, col_part(t, xo(-1), 0), xp)
                st["left"].wait_recv()
                left = same(t, col_part(t, xo(1), 1), xm)
                mates.append(same(t, col(t, xo(-1)), mate))
                mates.append(same(t, col(t, xo(1)), mate))
                st["right"], st["left"] = right, left
        else:
            st["right"].wait_recv()
            st["left"].wait_recv()
            mates.append(same(t, col(t, xo(2)), mate))
            st["up"].wait_recv()
            st["down"].wait_recv()
            mates.append(same(t, row(t, zo(NZ // 2)), mate))

    def close_chunk(t):
        for copy in state[t]["mates"]:
            copy.wait_recv()

    def amp_copy(d):
        target = lax.rem(g + d, GRP)
        return pltpu.make_async_remote_copy(
            src_ref=amps.at[:, target],
            dst_ref=sorted_amps.at[g],
            send_sem=amp_send.at[d],
            recv_sem=amp_recv.at[d],
            device_id=(y, target),
            device_id_type=MESH,
        )

    def start_amps(d, carry):
        amp_copy(d).start()
        return carry

    def wait_amps(d, carry):
        amp_copy(d).wait_recv()
        return carry

    def wait_amps_sent(d, carry):
        amp_copy(d).wait_send()
        return carry

    i_label = i_irrep[g]
    flips = [k_irrep[y * ks + kk] ^ i_label for kk in range(ks)]
    c_pos = lax.broadcasted_iota(jnp.int32, (rows, a), 0)

    def prepare(r, carry):
        for kk in range(ks):
            irrep = r ^ flips[kk]
            block = sorted_amps[pl.ds(irrep * subs, subs), kk].reshape(rows, a).astype(jnp.float32)
            live = jnp.where(c_pos < counts[irrep], block, 0.0)
            lhs[r, :, kk * rows : (kk + 1) * rows] = live.T.astype(lhs.dtype)
        return carry

    wide = NX * NZ * NC // n // NC
    split = NZ // wide

    def piece(r, held, kk):
        irrep = r ^ flips[kk]
        block = held[lax.div(irrep, split), pl.ds(lax.rem(irrep, split) * wide, wide), :, kk]
        return block.reshape(rows, b)

    def right_of(r, held):
        return jnp.concatenate([piece(r, held, kk) for kk in range(ks)], axis=0)

    def one(r, held):
        return jnp.dot(lhs[r], right_of(r, held), preferred_element_type=jnp.float32)

    def two(r, first, second):
        both = jnp.concatenate([right_of(r, first), right_of(r, second)], axis=1)
        return jnp.dot(lhs[r], both, preferred_element_type=jnp.float32)

    ups, downs = {}, {}

    def pass_on(table, source, dest, send_sem, recv_sem, s, h, step):
        copy = pltpu.make_async_remote_copy(
            src_ref=source.at[s, h],
            dst_ref=dest.at[s, h],
            send_sem=send_sem.at[s, h],
            recv_sem=recv_sem.at[s, h],
            device_id=(yo(step), g),
            device_id_type=MESH,
        )
        copy.start()
        table[s, h] = copy

    def upward(s, h):
        value = part[0, pl.ds(h * per, per)]
        if (s - 1, h) in ups:
            ups[s - 1, h].wait_recv()
            value = value + at_up[s - 1, h].astype(jnp.float32)
        to_up[s, h] = value.astype(to_up.dtype)
        pass_on(ups, to_up, at_up, send_up, recv_up, s, h, 1)

    def downward(s, h):
        value = part[1, pl.ds(h * per, per)]
        if (s - 1, h) in downs:
            downs[s - 1, h].wait_recv()
            value = value + at_down[s - 1, h].astype(jnp.float32)
        to_down[s, h] = value.astype(to_down.dtype)
        pass_on(downs, to_down, at_down, send_down, recv_down, s, h, -1)

    def products(s):
        def body(r, carry):
            both = two(r, lows[s], highs[s])
            part[0, r] = both[:, :b]
            part[1, r] = both[:, b:]
            return carry

        def body_one(r, carry):
            to_up[0, 0, r] = one(r, low0).astype(to_up.dtype)
            return carry

        def body_other(r, carry):
            to_down[0, 1, r] = one(r + per, low0).astype(to_down.dtype)
            return carry

        if s == 0:
            lax.fori_loop(0, per, body_one, 0)
            pass_on(ups, to_up, at_up, send_up, recv_up, 0, 0, 1)
            lax.fori_loop(0, per, body_other, 0)
            pass_on(downs, to_down, at_down, send_down, recv_down, 0, 1, -1)
            return
        lax.fori_loop(0, n, body, 0)
        for h in (1, 0) if s == 1 else (0, 1):
            upward(s, h)
            downward(s, 1 - h if s == 1 else h)

    open_chunk(0)
    lax.fori_loop(1, GRP, start_amps, 0)
    for t in range(1, far):
        open_chunk(t)
    for copy in own_blocks:
        copy.wait()
    steps = NZ // 2 + 1
    for turn in range(1, steps + far):
        if turn == steps:
            own_amps.wait()
            lax.fori_loop(1, GRP, wait_amps, 0)
            lax.fori_loop(0, n, prepare, 0)
        for t in range(far):
            if 1 <= turn - t <= steps:
                advance(t, turn - t)
        t = turn - steps - 1
        if t >= 0:
            close_chunk(t)
            products(t)
    close_chunk(far - 1)
    products(far - 1)

    def own(r, carry):
        part[0, r] = one(r, high0)
        return carry

    lax.fori_loop(0, n, own, 0)
    flip = i_label ^ j_irrep[y]
    a_pos = lax.broadcasted_iota(jnp.int32, (a, b), 0)
    b_pos = lax.broadcasted_iota(jnp.int32, (a, b), 1)
    for h in (0, 1):
        ups[far - 1, h].wait_recv()
        downs[far - 1, h].wait_recv()

        def total(r, carry):
            irrep = r + h * per
            value = part[0, irrep] + at_up[far - 1, h, r].astype(jnp.float32) + at_down[far - 1, h, r].astype(jnp.float32)
            live = (a_pos < counts[irrep]) & (b_pos < counts[irrep ^ flip])
            masked = jnp.where(live, value, 0.0).astype(summed.dtype)
            summed[pl.ds(irrep * subs, subs)] = masked.reshape(subs, c, b)
            return carry

        lax.fori_loop(0, per, total, 0)

    def out_copy(d):
        target = lax.rem(g + d, GRP)
        return pltpu.make_async_remote_copy(
            src_ref=summed.at[target],
            dst_ref=out.at[g],
            send_sem=out_send.at[d],
            recv_sem=out_recv.at[d],
            device_id=(y, target),
            device_id_type=MESH,
        )

    def start_out(d, carry):
        out_copy(d).start()
        return carry

    def wait_out(d, carry):
        out_copy(d).wait_recv()
        out_copy(d).wait_send()
        return carry

    lax.fori_loop(1, GRP, start_out, 0)
    own_out = pltpu.make_async_copy(summed.at[g], out.at[g], local_sem.at[0])
    own_out.start()
    lax.fori_loop(1, GRP, wait_amps_sent, 0)
    for _, copy in started:
        copy.wait_send()
    for copy in list(ups.values()) + list(downs.values()):
        copy.wait_send()
    own_out.wait()
    lax.fori_loop(1, GRP, wait_out, 0)


def shards(amps, cycle_inter, k_irrep, i_irrep, j_irrep, virt_count):
    ks, i_total, c, a = amps.shape
    j, b = cycle_inter.shape[2:]
    n = virt_count.shape[0]
    half = (j // 2, 2, n // 2, a, b)
    turned = jnp.transpose(cycle_inter, (2, 0, 1, 3))
    dma = pltpu.SemaphoreType.DMA
    out = pl.pallas_call(
        cycle_kernel,
        out_shape=jax.ShapeDtypeStruct((i_total, c, b), jnp.bfloat16),
        in_specs=[pl.BlockSpec(memory_space=pltpu.SMEM)] * 4
        + [pl.BlockSpec(memory_space=pl.ANY), pl.BlockSpec(memory_space=pltpu.VMEM)],
        out_specs=pl.BlockSpec(memory_space=pl.ANY),
        scratch_shapes=[pltpu.VMEM((NX, NZ, NC, ks, c, b), jnp.bfloat16)] * j
        + [
            pltpu.VMEM((GRP, ks, c, a), jnp.bfloat16),
            pltpu.VMEM((n, a, ks * a), jnp.bfloat16),
            pltpu.VMEM((2, n, a, b), jnp.float32),
            pltpu.VMEM((GRP, c, b), jnp.bfloat16),
        ]
        + [pltpu.VMEM(half, jnp.bfloat16)] * 4
        + [dma((j + 1,))]
        + [dma((COPIES * j // 2,))] * 2
        + [dma((GRP,))] * 4
        + [dma(half[:2])] * 4,
        compiler_params=pltpu.CompilerParams(collective_id=0, has_side_effects=True, vmem_limit_bytes=48 << 20),
    )(k_irrep, i_irrep, j_irrep, virt_count, amps, turned)
    return out.reshape(i_total, 1, c, b)


def solution(mesh):
    return jax.shard_map(
        shards,
        mesh=mesh,
        in_specs=(P("batch", None, "grp", None), P("batch", "grp", None, None), P(), P(), P(), P()),
        out_specs=P(None, "batch", "grp", None),
        check_vma=False,
    )
```

```python
import jax
import jax.numpy as jnp
from jax import lax
from jax.experimental import pallas as pl
from jax.experimental.pallas import tpu as pltpu
from jax.sharding import PartitionSpec as P

MESH = pl.DeviceIdType.MESH
NX, NZ, NC = 4, 8, 2
GRP = NX * NZ * NC
COPIES = 34


def cycle_kernel(
    k_irrep, i_irrep, j_irrep, counts, amps, src, out,
    low0, low1, low2, low3, high0, high1, high2, high3, sorted_amps, lhs, part, summed, to_up, at_up, to_down, at_down,
    local_sem, send, recv, amp_send, amp_recv, out_send, out_recv, send_up, recv_up, send_down, recv_down,
):
    y, g = lax.axis_index("batch"), lax.axis_index("grp")
    core = lax.rem(g, NC)
    z = lax.rem(lax.div(g, NC), NZ)
    x = lax.div(g, NC * NZ)
    lows, highs = (low0, low1, low2, low3), (high0, high1, high2, high3)
    _, _, _, ks, c, b = low0.shape
    ring = src.shape[0]
    far = ring // 2
    n, a = lhs.shape[:2]
    rows = lhs.shape[2] // ks
    subs = rows // c
    per = n // 2

    def yo(d):
        return lax.rem(y + d + ring, ring)

    def xo(d):
        return lax.rem(x + d + NX, NX)

    def zo(d):
        return lax.rem(z + d + NZ, NZ)

    def dev(xx, zz, cc):
        return (y, (xx * NZ + zz) * NC + cc)

    def low(t):
        return yo(far - t)

    def high(t):
        return y if t == 0 else yo(t - far)

    own_blocks = []
    for t in range(far):
        for side, (j, held) in enumerate(((low(t), lows[t]), (high(t), highs[t]))):
            own_blocks.append(pltpu.make_async_copy(src.at[j], held.at[x, z, core], local_sem.at[2 * t + side]))
    own_amps = pltpu.make_async_copy(amps.at[:, g], sorted_amps.at[g], local_sem.at[ring])
    for copy in own_blocks + [own_amps]:
        copy.start()

    barrier = pltpu.get_barrier_semaphore()

    def greet(d, carry):
        pl.semaphore_signal(barrier, inc=1, device_id=(y, lax.rem(g + d, GRP)), device_id_type=MESH)
        return carry

    lax.fori_loop(1, GRP, greet, 0)
    for d in (1, -1):
        pl.semaphore_signal(barrier, inc=1, device_id=(yo(d), g), device_id_type=MESH)
    pl.semaphore_wait(barrier, GRP + 1)

    started = []

    def go(t, view, at, target):
        table = [p for p in started if p[0] == t]
        at_sem = t * COPIES + len(table)
        copy = pltpu.make_async_remote_copy(
            src_ref=view, dst_ref=at, send_sem=send.at[at_sem], recv_sem=recv.at[at_sem], device_id=target, device_id_type=MESH
        )
        copy.start()
        started.append((t, copy))
        return copy

    def same(t, ref, target):
        return go(t, ref, ref, target)

    def row(t, zz):
        return lows[t].at[:, zz, core]

    def row_part(t, zz, p):
        return lows[t].at[pl.ds(p * (NX // 2), NX // 2), zz, core]

    def col(t, xx):
        return highs[t].at[xx, :, core]

    def col_part(t, xx, p):
        return highs[t].at[xx, pl.ds(p * (NZ // 2), NZ // 2), core]

    mate = dev(x, z, 1 - core)
    zp, zm = dev(x, zo(1), core), dev(x, zo(-1), core)
    xp, xm = dev(xo(1), z, core), dev(xo(-1), z, core)
    state = {}

    def open_chunk(t):
        along_x = [go(t, src.at[low(t)], lows[t].at[x, z, core], dev(xo(d), z, core)) for d in range(1, NX)]
        along_z = [go(t, src.at[high(t)], highs[t].at[x, z, core], dev(x, zo(d), core)) for d in range(1, NZ)]
        state[t] = dict(along_x=along_x, along_z=along_z, mates=[])

    def advance(t, step):
        st = state[t]
        mates = st["mates"]
        if step == 1:
            for copy in st["along_x"]:
                copy.wait_recv()
            st["up"] = same(t, row(t, z), zp)
            st["down"] = same(t, row(t, z), zm)
            for copy in st["along_z"]:
                copy.wait_recv()
            st["right"] = same(t, col(t, x), xp)
            st["left"] = same(t, col(t, x), xm)
            mates.append(same(t, row(t, z), mate))
            mates.append(same(t, col(t, x), mate))
        elif step <= NZ // 2:
            s = step - 1
            last = s == NZ // 2 - 1
            st["up"].wait_recv()
            up = same(t, row_part(t, zo(-s), 0) if last else row(t, zo(-s)), zp)
            st["down"].wait_recv()
            down = same(t, row_part(t, zo(s), 1) if last else row(t, zo(s)), zm)
            mates.append(same(t, row(t, zo(-s)), mate))
            mates.append(same(t, row(t, zo(s)), mate))
            st["up"], st["down"] = up, down
            if s == 2:
                st["right"].wait_recv()
                right = same(t, col_part(t, xo(-1), 0), xp)
                st["left"].wait_recv()
                left = same(t, col_part(t, xo(1), 1), xm)
                mates.append(same(t, col(t, xo(-1)), mate))
                mates.append(same(t, col(t, xo(1)), mate))
                st["right"], st["left"] = right, left
        else:
            st["right"].wait_recv()
            st["left"].wait_recv()
            mates.append(same(t, col(t, xo(2)), mate))
            st["up"].wait_recv()
            st["down"].wait_recv()
            mates.append(same(t, row(t, zo(NZ // 2)), mate))

    def close_chunk(t):
        for copy in state[t]["mates"]:
            copy.wait_recv()

    def amp_copy(d):
        target = lax.rem(g + d, GRP)
        return pltpu.make_async_remote_copy(
            src_ref=amps.at[:, target],
            dst_ref=sorted_amps.at[g],
            send_sem=amp_send.at[d],
            recv_sem=amp_recv.at[d],
            device_id=(y, target),
            device_id_type=MESH,
        )

    def start_amps(d, carry):
        amp_copy(d).start()
        return carry

    def wait_amps(d, carry):
        amp_copy(d).wait_recv()
        return carry

    def wait_amps_sent(d, carry):
        amp_copy(d).wait_send()
        return carry

    i_label = i_irrep[g]
    flips = [k_irrep[y * ks + kk] ^ i_label for kk in range(ks)]
    c_pos = lax.broadcasted_iota(jnp.int32, (rows, a), 0)

    def prepare(r, carry):
        for kk in range(ks):
            irrep = r ^ flips[kk]
            block = sorted_amps[pl.ds(irrep * subs, subs), kk].reshape(rows, a).astype(jnp.float32)
            live = jnp.where(c_pos < counts[irrep], block, 0.0)
            lhs[r, :, kk * rows : (kk + 1) * rows] = live.T.astype(lhs.dtype)
        return carry

    wide = NX * NZ * NC // n // NC
    split = NZ // wide

    def piece(r, held, kk):
        irrep = r ^ flips[kk]
        block = held[lax.div(irrep, split), pl.ds(lax.rem(irrep, split) * wide, wide), :, kk]
        return block.reshape(rows, b)

    def right_of(r, held):
        return jnp.concatenate([piece(r, held, kk) for kk in range(ks)], axis=0)

    def one(r, held):
        return jnp.dot(lhs[r], right_of(r, held), preferred_element_type=jnp.float32)

    def two(r, first, second):
        both = jnp.concatenate([right_of(r, first), right_of(r, second)], axis=1)
        return jnp.dot(lhs[r], both, preferred_element_type=jnp.float32)

    ups, downs = {}, {}

    def pass_on(table, source, dest, send_sem, recv_sem, s, h, step):
        copy = pltpu.make_async_remote_copy(
            src_ref=source.at[s, h],
            dst_ref=dest.at[s, h],
            send_sem=send_sem.at[s, h],
            recv_sem=recv_sem.at[s, h],
            device_id=(yo(step), g),
            device_id_type=MESH,
        )
        copy.start()
        table[s, h] = copy

    def upward(s, h):
        value = part[0, pl.ds(h * per, per)]
        if (s - 1, h) in ups:
            ups[s - 1, h].wait_recv()
            value = value + at_up[s - 1, h].astype(jnp.float32)
        to_up[s, h] = value.astype(to_up.dtype)
        pass_on(ups, to_up, at_up, send_up, recv_up, s, h, 1)

    def downward(s, h):
        value = part[1, pl.ds(h * per, per)]
        if (s - 1, h) in downs:
            downs[s - 1, h].wait_recv()
            value = value + at_down[s - 1, h].astype(jnp.float32)
        to_down[s, h] = value.astype(to_down.dtype)
        pass_on(downs, to_down, at_down, send_down, recv_down, s, h, -1)

    def products(s):
        def body(r, carry):
            both = two(r, lows[s], highs[s])
            part[0, r] = both[:, :b]
            part[1, r] = both[:, b:]
            return carry

        def body_one(r, carry):
            to_up[0, 0, r] = one(r, low0).astype(to_up.dtype)
            return carry

        def body_other(r, carry):
            to_down[0, 1, r] = one(r + per, low0).astype(to_down.dtype)
            return carry

        if s == 0:
            lax.fori_loop(0, per, body_one, 0)
            pass_on(ups, to_up, at_up, send_up, recv_up, 0, 0, 1)
            lax.fori_loop(0, per, body_other, 0)
            pass_on(downs, to_down, at_down, send_down, recv_down, 0, 1, -1)
            return
        lax.fori_loop(0, n, body, 0)
        for h in (1, 0) if s == 1 else (0, 1):
            upward(s, h)
            downward(s, 1 - h if s == 1 else h)

    open_chunk(0)
    lax.fori_loop(1, GRP, start_amps, 0)
    for copy in own_blocks:
        copy.wait()
    steps = NZ // 2 + 1
    lag = 1
    for turn in range(1, steps + lag * (far - 1) + 2):
        for t in range(far):
            step = turn - lag * t
            if step == 0:
                open_chunk(t)
            elif 1 <= step <= steps:
                advance(t, step)
        for t in range(far):
            if turn - lag * t == steps + 1:
                if t == 0:
                    own_amps.wait()
                    lax.fori_loop(1, GRP, wait_amps, 0)
                    lax.fori_loop(0, n, prepare, 0)
                close_chunk(t)
                products(t)

    def own(r, carry):
        part[0, r] = one(r, high0)
        return carry

    lax.fori_loop(0, n, own, 0)
    flip = i_label ^ j_irrep[y]
    a_pos = lax.broadcasted_iota(jnp.int32, (a, b), 0)
    b_pos = lax.broadcasted_iota(jnp.int32, (a, b), 1)
    for h in (0, 1):
        ups[far - 1, h].wait_recv()
        downs[far - 1, h].wait_recv()

        def total(r, carry):
            irrep = r + h * per
            value = part[0, irrep] + at_up[far - 1, h, r].astype(jnp.float32) + at_down[far - 1, h, r].astype(jnp.float32)
            live = (a_pos < counts[irrep]) & (b_pos < counts[irrep ^ flip])
            masked = jnp.where(live, value, 0.0).astype(summed.dtype)
            summed[pl.ds(irrep * subs, subs)] = masked.reshape(subs, c, b)
            return carry

        lax.fori_loop(0, per, total, 0)

    def out_copy(d):
        target = lax.rem(g + d, GRP)
        return pltpu.make_async_remote_copy(
            src_ref=summed.at[target],
            dst_ref=out.at[g],
            send_sem=out_send.at[d],
            recv_sem=out_recv.at[d],
            device_id=(y, target),
            device_id_type=MESH,
        )

    def start_out(d, carry):
        out_copy(d).start()
        return carry

    def wait_out(d, carry):
        out_copy(d).wait_recv()
        out_copy(d).wait_send()
        return carry

    lax.fori_loop(1, GRP, start_out, 0)
    own_out = pltpu.make_async_copy(summed.at[g], out.at[g], local_sem.at[0])
    own_out.start()
    lax.fori_loop(1, GRP, wait_amps_sent, 0)
    for _, copy in started:
        copy.wait_send()
    for copy in list(ups.values()) + list(downs.values()):
        copy.wait_send()
    own_out.wait()
    lax.fori_loop(1, GRP, wait_out, 0)


def shards(amps, cycle_inter, k_irrep, i_irrep, j_irrep, virt_count):
    ks, i_total, c, a = amps.shape
    j, b = cycle_inter.shape[2:]
    n = virt_count.shape[0]
    half = (j // 2, 2, n // 2, a, b)
    turned = jnp.transpose(cycle_inter, (2, 0, 1, 3))
    dma = pltpu.SemaphoreType.DMA
    out = pl.pallas_call(
        cycle_kernel,
        out_shape=jax.ShapeDtypeStruct((i_total, c, b), jnp.bfloat16),
        in_specs=[pl.BlockSpec(memory_space=pltpu.SMEM)] * 4
        + [pl.BlockSpec(memory_space=pl.ANY), pl.BlockSpec(memory_space=pltpu.VMEM)],
        out_specs=pl.BlockSpec(memory_space=pl.ANY),
        scratch_shapes=[pltpu.VMEM((NX, NZ, NC, ks, c, b), jnp.bfloat16)] * j
        + [
            pltpu.VMEM((GRP, ks, c, a), jnp.bfloat16),
            pltpu.VMEM((n, a, ks * a), jnp.bfloat16),
            pltpu.VMEM((2, n, a, b), jnp.float32),
            pltpu.VMEM((GRP, c, b), jnp.bfloat16),
        ]
        + [pltpu.VMEM(half, jnp.bfloat16)] * 4
        + [dma((j + 1,))]
        + [dma((COPIES * j // 2,))] * 2
        + [dma((GRP,))] * 4
        + [dma(half[:2])] * 4,
        compiler_params=pltpu.CompilerParams(collective_id=0, has_side_effects=True, vmem_limit_bytes=48 << 20),
    )(k_irrep, i_irrep, j_irrep, virt_count, amps, turned)
    return out.reshape(i_total, 1, c, b)


def solution(mesh):
    return jax.shard_map(
        shards,
        mesh=mesh,
        in_specs=(P("batch", None, "grp", None), P("batch", "grp", None, None), P(), P(), P(), P()),
        out_specs=P(None, "batch", "grp", None),
        check_vma=False,
    )
```
